32 devices in a mesh: job: 2 (over x), tok: 16 (over z, y, core).
Axes of the slice: x: 2, y: 2, z: 4, core: 2. Of those that a mesh axis runs over, the one named last changes fastest.
Arguments:
- pair_states: bfloat16 [1024, 512, 128], P(('job', 'tok')), parts along dimension 0, may hold values from -6 to 6
- weight_in: bfloat16 [128, 1024], replicated, may hold values from -0.5 to 0.5
- weight_out: bfloat16 [512, 128], replicated, may hold values from -0.25 to 0.25
- weight_bias: bfloat16 [2, 128, 16], replicated, may hold values from -0.5 to 0.5
- key_mask: int32 [1024], P('job'), parts along dimension 0, may hold values 0 or 1
- noise_level: int32 [4], P('job'), parts along dimension 0, may hold values from 0 to 199
- query_states: bfloat16 [2, 16, 4, 48, 512], P(None, 'tok', 'job'), parts along dimension 2, may hold values from -16 to 16
- key_states: bfloat16 [2, 16, 4, 48, 512], P(None, 'tok', 'job'), parts along dimension 2, may hold values from -16 to 16
- value_states: bfloat16 [2, 16, 4, 48, 512], P(None, 'tok', 'job'), parts along dimension 2, may hold values from -6 to 6
- output_grad: bfloat16 [2, 16, 4, 48, 512], P(None, 'tok', 'job'), parts along dimension 2, may hold values from -6 to 6
Outputs:
- pair_grad: bfloat16 [1024, 512, 128], P(('job', 'tok')), parts along dimension 0
- query_grad: bfloat16 [2, 16, 4, 48, 512], P(None, 'tok', 'job'), parts along dimension 2
- key_grad: bfloat16 [2, 16, 4, 48, 512], P(None, 'tok', 'job'), parts along dimension 2
- value_grad: bfloat16 [2, 16, 4, 48, 512], P(None, 'tok', 'job'), parts along dimension 2
- weight_in_grad: float32 [256, 1024], P('job'), parts along dimension 0
- weight_out_grad: float32 [1024, 128], P('job'), parts along dimension 0
- weight_bias_grad: float32 [4, 128, 16], P('job'), parts along dimension 0
The draws below stay inside these ranges and needn't reach their ends.
There are 2 independent parts, one for each index of `job`. The reference program is written for one: setup_inputs(seed, part) draws one part's arguments, and reference() takes and returns one part's arrays. A program takes and returns all parts, laid end to end along the dimension named above; an argument that names none is the same for every part. Nothing has to cross between parts.
All inputs are finite; a program needn't handle non-finite values.
Results may differ from the reference program's by a relative error of at most 0.015.
Values may be sent and summed in bfloat16 or wider, within the bound.
A program may use at most 192 MiB of HBM per device.

```python
import math
import jax
import jax.numpy as jnp
from jax import lax

CZ = 128
FF = 512
H = 16
DH = 48
N = 512
BLOCKS = 2
LEVELS = 200
S_DEV = 2
GH = 16
SAMPLES = 2


def query_key(key):
    base = jax.random.fold_in(key, 4099)
    seed_query, seed_key = jax.random.split(base, 2)
    shape = (BLOCKS, GH, S_DEV, DH, N)
    query_draw = jnp.clip(jax.random.normal(seed_query, shape, jnp.float32), -6.0, 6.0)
    key_draw = jnp.clip(jax.random.normal(seed_key, shape, jnp.float32), -6.0, 6.0)
    return (query_draw, key_draw)


def draw_query_states(key, part):
    return query_key(key)[0].astype(jnp.bfloat16)


def draw_key_states(key, part):
    return query_key(key)[1].astype(jnp.bfloat16)


def with_ends(values, stream_key, least, high):
    place = [jax.random.randint(jax.random.fold_in(stream_key, axis), (), 0, length) for axis, length in enumerate(values.shape)]
    main_axis = values.shape.index(max(values.shape))
    next_to = place[:main_axis] + [(place[main_axis] + 1) % values.shape[main_axis]] + place[main_axis + 1:]
    return values.at[tuple(place)].set(least).at[tuple(next_to)].set(high)


def steps_of(own_key, shape, cuts, least, largest):
    level = 1.0
    for dim, blocks in cuts:
        heights = jax.random.uniform(jax.random.fold_in(jax.random.fold_in(own_key, 6), dim), (blocks,), jnp.float32, least / len(cuts), largest / len(cuts))
        level = level * jnp.repeat(jnp.exp(heights), shape[dim] // blocks).reshape((-1,) + (1,) * (len(shape) - 1 - dim))
    return level


def gaussian(key, dims, deviation, bound, cuts=(), kind=jnp.bfloat16):
    drawn = jax.random.normal(key, dims, jnp.float32) * deviation
    if len(cuts) > 0:
        drawn = steps_of(key, dims, cuts, -0.22, 0.18) * drawn
    return jnp.clip(drawn, min=-bound, max=bound).astype(kind)


def setup_inputs(seed: int = 0, part: int = 0) -> dict:
    splits = jax.random.split(jax.random.key(seed), 11)
    part_keys = jax.random.split(jax.random.fold_in(splits[10], part), 11)
    return {
        "pair_states": gaussian(part_keys[0], (N, N, CZ), 1.0, 6.0, ((0, 16),)),
        "weight_in": gaussian(splits[1], (CZ, 2 * FF), CZ ** -0.5, 0.5),
        "weight_out": gaussian(splits[2], (FF, CZ), FF ** -0.5, 0.25),
        "weight_bias": gaussian(splits[3], (BLOCKS, CZ, H), CZ ** -0.5, 0.5),
        "key_mask": with_ends((jax.random.randint(part_keys[4], (N,), 0, 8) < 7).astype(jnp.int32), jax.random.fold_in(part_keys[4], 1), 0, 1),
        "noise_level": jax.random.randint(part_keys[5], (SAMPLES,), 0, LEVELS).astype(jnp.int32),
        "query_states": draw_query_states(jax.random.fold_in(jax.random.fold_in(splits[10], part), 71), part),
        "key_states": draw_key_states(jax.random.fold_in(jax.random.fold_in(splits[10], part), 71), part),
        "value_states": gaussian(part_keys[8], (BLOCKS, GH, S_DEV, DH, N), 1.0, 6.0, ((1, 16),)),
        "output_grad": gaussian(part_keys[9], (BLOCKS, GH, S_DEV, DH, N), 1.0, 6.0, ((1, 16),)),
    }


sigma_high = 160.0
sigma_low = 0.0004
sigma_data = 16.0
rho_power = 7.0
epsilon = 1e-05
masked_score = -1000000000.0

def sample_weight(levels):
    level = levels.astype(jnp.float32)
    top_root = sigma_high ** (1.0 / rho_power)
    low_root = sigma_low ** (1.0 / rho_power)
    sigma_level = (top_root + level / (LEVELS - 1) * (low_root - top_root)) ** rho_power
    return (sigma_level * sigma_level + sigma_data * sigma_data) / (sigma_level + sigma_data) ** 2

def normalize(inputs):
    row_mean = lax.optimization_barrier(jnp.mean(inputs, -1, keepdims=True))
    centered = inputs - row_mean
    variance = lax.optimization_barrier(jnp.mean(centered * centered, -1, keepdims=True))
    inv_std = lax.rsqrt(variance + epsilon)
    return (centered * inv_std, inv_std)

def norm_back(inputs, upstream):
    normed, inv_std = normalize(inputs)
    return inv_std * (upstream - lax.optimization_barrier(jnp.mean(upstream, -1, keepdims=True)) - normed * lax.optimization_barrier(jnp.mean(upstream * normed, -1, keepdims=True)))

def tile_forward(flattened, weight_in, weight_out):
    hidden_width = weight_out.shape[0]
    pair_float = flattened.astype(jnp.float32)
    normed_in = normalize(pair_float)[0].astype(jnp.bfloat16)
    projected = jnp.dot(normed_in, weight_in, preferred_element_type=jnp.float32)
    gate_in = projected[:, :hidden_width]
    up_in = projected[:, hidden_width:]
    hidden = (jax.nn.silu(gate_in) * up_in).astype(jnp.bfloat16)
    lifted = pair_float + jnp.dot(hidden, weight_out, preferred_element_type=jnp.float32)
    normed_out = normalize(lifted)[0].astype(jnp.bfloat16)
    return (pair_float, normed_in, gate_in, up_in, hidden, lifted, normed_out)

def tile_backward(stored, bias_half, weight_in, weight_out, weight_bias):
    pair_float, normed_in, gate_in, up_in, hidden, lifted, normed_out = stored
    bias_float = bias_half.astype(jnp.float32)
    d_normed = jnp.einsum('bhp,bch->pc', bias_float, weight_bias.astype(jnp.float32))
    grad_bias = jnp.einsum('pc,bhp->bch', normed_out.astype(jnp.float32), bias_float)
    d_lifted = norm_back(lifted, d_normed)
    lifted_half = d_lifted.astype(jnp.bfloat16)
    grad_out = jnp.einsum('pf,pc->fc', hidden.astype(jnp.float32), lifted_half.astype(jnp.float32))
    d_hidden = jnp.dot(lifted_half, weight_out.T, preferred_element_type=jnp.float32)
    gate_sigmoid = jax.nn.sigmoid(gate_in)
    d_gate = d_hidden * up_in * gate_sigmoid * (1.0 + gate_in * (1.0 - gate_sigmoid))
    d_up = d_hidden * gate_in * gate_sigmoid
    d_projected = jnp.concatenate([d_gate, d_up], -1).astype(jnp.bfloat16)
    grad_in = jnp.einsum('pc,pf->cf', normed_in.astype(jnp.float32), d_projected.astype(jnp.float32))
    d_normed_in = jnp.dot(d_projected, weight_in.T, preferred_element_type=jnp.float32)
    pair_grad = (d_lifted + norm_back(pair_float, d_normed_in)).astype(jnp.bfloat16)
    return (pair_grad, grad_in, grad_out, grad_bias)

def sample_back(query_vec, key_vec, value_vec, upstream, bias_float, key_valid, weight):
    scaling = 1.0 / math.sqrt(query_vec.shape[0])
    raw_scores = jnp.einsum('di,dj->ij', query_vec.astype(jnp.float32), key_vec.astype(jnp.float32)) * scaling + bias_float
    raw_scores = jnp.where(key_valid[None, :], raw_scores, masked_score)
    row_peak = lax.optimization_barrier(jnp.max(raw_scores, -1, keepdims=True))
    exp_scores = jnp.exp(raw_scores - row_peak)
    attention = exp_scores / lax.optimization_barrier(jnp.sum(exp_scores, -1, keepdims=True))
    attention_half = attention.astype(jnp.bfloat16)
    grad_half = (weight * upstream.astype(jnp.float32)).astype(jnp.bfloat16)
    d_attention = jnp.einsum('di,dj->ij', grad_half.astype(jnp.float32), value_vec.astype(jnp.float32))
    d_scores = attention * (d_attention - lax.optimization_barrier(jnp.sum(attention * d_attention, -1, keepdims=True)))
    scores_half = d_scores.astype(jnp.bfloat16)
    d_value = jnp.einsum('ij,di->dj', attention_half.astype(jnp.float32), grad_half.astype(jnp.float32)).astype(jnp.bfloat16)
    d_query = (jnp.einsum('ij,dj->di', scores_half.astype(jnp.float32), key_vec.astype(jnp.float32)) * scaling).astype(jnp.bfloat16)
    d_key = (jnp.einsum('ij,di->dj', scores_half.astype(jnp.float32), query_vec.astype(jnp.float32)) * scaling).astype(jnp.bfloat16)
    return (d_query, d_key, d_value, d_scores)

def attend_block(queries, keys_in, values_in, grads_in, bias_float, key_valid, weights):

    def advance(summed, items):
        query_vec, key_vec, value_vec, upstream, weight = items
        d_query, d_key, d_value, d_scores = sample_back(query_vec, key_vec, value_vec, upstream, bias_float, key_valid, weight)
        return (summed + d_scores, (d_query, d_key, d_value))
    start = jnp.zeros((queries.shape[2], queries.shape[2]), jnp.float32)
    return lax.scan(advance, start, (queries, keys_in, values_in, grads_in, weights))

def reference(pair_states, weight_in, weight_out, weight_bias, key_mask, noise_level, query_states, key_states, value_states, output_grad):
    row_block = N // 16
    rows_all = pair_states.reshape(16, row_block * N, CZ)

    def forward_rows(flattened):
        normed_out = tile_forward(flattened, weight_in, weight_out)[6]
        return jnp.einsum('pc,bch->bhp', normed_out.astype(jnp.float32), weight_bias.astype(jnp.float32)).astype(jnp.bfloat16)
    biases = lax.map(forward_rows, rows_all)
    biases = jnp.transpose(biases, (1, 2, 0, 3)).reshape(BLOCKS, H, N, N)
    key_valid = key_mask > 0
    weights_all = sample_weight(noise_level)
    slots = query_states.shape[1]

    def per_slot(flat_index):
        layer = flat_index // slots
        slot = flat_index % slots
        bias_float = biases[layer, slot % H].astype(jnp.float32)
        weights = lax.dynamic_slice_in_dim(weights_all, slot // H * S_DEV, S_DEV)
        return attend_block(query_states[layer, slot], key_states[layer, slot], value_states[layer, slot], output_grad[layer, slot], bias_float, key_valid, weights)
    summed, (d_query, d_key, d_value) = lax.map(per_slot, jnp.arange(BLOCKS * slots, dtype=jnp.int32))
    bias_grad = lax.optimization_barrier(jnp.sum(summed.reshape(BLOCKS, slots // H, H, N, N), 1))
    bias_half = bias_grad.astype(jnp.bfloat16)
    bias_rows = jnp.transpose(bias_half.reshape(BLOCKS, H, 16, row_block * N), (2, 0, 1, 3))

    def backward_rows(carry, items):
        flattened, bias_piece = items
        stored = tile_forward(flattened, weight_in, weight_out)
        pair_grad, grad_in, grad_out, grad_bias = tile_backward(stored, bias_piece, weight_in, weight_out, weight_bias)
        return ((carry[0] + grad_in, carry[1] + grad_out, carry[2] + grad_bias), pair_grad)
    start = (jnp.zeros((CZ, 2 * FF), jnp.float32), jnp.zeros((FF, CZ), jnp.float32), jnp.zeros((BLOCKS, CZ, H), jnp.float32))
    (grad_in, grad_out, grad_bias), pair_rows = lax.scan(backward_rows, start, (rows_all, bias_rows))
    pair_grad = pair_rows.reshape(N, N, CZ)
    shape = (BLOCKS, slots, S_DEV, DH, N)
    return (pair_grad, d_query.reshape(shape), d_key.reshape(shape), d_value.reshape(shape), grad_in, grad_out, grad_bias)
```

```python
import functools
import math

import jax
import jax.numpy as jnp
from jax import lax
from jax.experimental import pallas as pl
from jax.experimental.pallas import tpu as pltpu
from jax.sharding import PartitionSpec as P

LEVELS = 200
CHUNKS = 2
VMEM_LIMIT = 56 * 1024 * 1024

sigma_high = 160.0
sigma_low = 0.0004
sigma_data = 16.0
rho_power = 7.0
epsilon = 1e-05
masked_score = -1000000000.0

F32 = jnp.float32
BF16 = jnp.bfloat16


def sample_weight(levels):
    level = levels.astype(F32)
    top_root = sigma_high ** (1.0 / rho_power)
    low_root = sigma_low ** (1.0 / rho_power)
    sigma_level = (top_root + level / (LEVELS - 1) * (low_root - top_root)) ** rho_power
    return (sigma_level * sigma_level + sigma_data * sigma_data) / (sigma_level + sigma_data) ** 2


def normalize(inputs):
    row_mean = jnp.mean(inputs, -1, keepdims=True)
    centered = inputs - row_mean
    variance = jnp.mean(centered * centered, -1, keepdims=True)
    inv_std = lax.rsqrt(variance + epsilon)
    return (centered * inv_std, inv_std)


def norm_back(normed, inv_std, upstream):
    return inv_std * (
        upstream
        - jnp.mean(upstream, -1, keepdims=True)
        - normed * jnp.mean(upstream * normed, -1, keepdims=True)
    )


def mm(a, b, ca, cb):
    return lax.dot_general(a, b, (((ca,), (cb,)), ((), ())), preferred_element_type=F32)


def sigmoid(x):
    return 0.5 * jnp.tanh(0.5 * x) + 0.5


def forward_kernel(pair_ref, win_ref, wout_ref, wb_ref, bias_ref):
    width = wout_ref.shape[0]
    for r in range(pair_ref.shape[0]):
        pair_float = pair_ref[r].astype(F32)
        normed_in = normalize(pair_float)[0].astype(BF16)
        projected = mm(normed_in, win_ref[...], 1, 0)
        gate = projected[:, :width]
        hidden = (gate * sigmoid(gate) * projected[:, width:]).astype(BF16)
        lifted = pair_float + mm(hidden, wout_ref[...], 1, 0)
        normed_out = normalize(lifted)[0].astype(BF16)
        bias_ref[r] = mm(wb_ref[...], normed_out, 1, 1).astype(BF16)


def forward_rows(pair_states, win, wout, wb, chunk, chunks, step):
    rows, n, cz = pair_states.shape
    count = rows // chunks
    step = min(step, count)
    first = chunk * (count // step)
    heads = wb.shape[0]
    return pl.pallas_call(
        forward_kernel,
        name=f"pair_forward_{chunk}",
        grid=(count // step,),
        in_specs=[
            pl.BlockSpec((step, n, cz), lambda i: (first + i, 0, 0)),
            pl.BlockSpec(win.shape, lambda i: (0, 0)),
            pl.BlockSpec(wout.shape, lambda i: (0, 0)),
            pl.BlockSpec(wb.shape, lambda i: (0, 0)),
        ],
        out_specs=pl.BlockSpec((step, heads, n), lambda i: (i, 0, 0)),
        out_shape=jax.ShapeDtypeStruct((count, heads, n), BF16),
        compiler_params=pltpu.CompilerParams(vmem_limit_bytes=VMEM_LIMIT),
        cost_estimate=pl.CostEstimate(
            flops=2 * count * n * cz * (3 * wout.shape[0] + heads) * 2,
            bytes_accessed=count * n * (cz + heads) * 2,
            transcendentals=count * n * wout.shape[0],
        ),
    )(pair_states, win, wout, wb)


def backward_kernel(pair_ref, bias_ref, win_ref, wout_ref, wint_ref, woutt_ref, wb_ref, *rest):
    out_ref, acc_ref = rest[-2:]
    width = wout_ref.shape[0]
    heads = wb_ref.shape[0]

    @pl.when(pl.program_id(0) == 0)
    def _():
        if len(rest) == 4:
            acc_ref[...] = rest[0][...]
        else:
            acc_ref[...] = jnp.zeros_like(acc_ref)

    for r in range(pair_ref.shape[0]):
        pair_float = pair_ref[r].astype(F32)
        xhat, inv_in = normalize(pair_float)
        normed_in = xhat.astype(BF16)
        projected = mm(normed_in, win_ref[...], 1, 0)
        gate = projected[:, :width]
        up = projected[:, width:]
        sg = sigmoid(gate)
        act = gate * sg
        hidden = (act * up).astype(BF16)
        lifted = pair_float + mm(hidden, wout_ref[...], 1, 0)
        yhat, inv_out = normalize(lifted)
        normed_out = yhat.astype(BF16)
        bias = bias_ref[r]
        d_normed = mm(bias, wb_ref[...], 0, 0)
        d_lifted = norm_back(yhat, inv_out, d_normed)
        lifted_half = d_lifted.astype(BF16)
        d_hidden = mm(lifted_half, woutt_ref[...], 1, 0)
        d_gate = (d_hidden * up * (sg + act * (1.0 - sg))).astype(BF16)
        d_up = (d_hidden * act).astype(BF16)
        d_normed_in = mm(d_gate, wint_ref[:width], 1, 0) + mm(d_up, wint_ref[width:], 1, 0)
        out_ref[r] = (d_lifted + norm_back(xhat, inv_in, d_normed_in)).astype(BF16)
        acc_ref[:, :width] += mm(normed_in, d_gate, 0, 0)
        acc_ref[:, width : 2 * width] += mm(normed_in, d_up, 0, 0)
        acc_ref[:, 2 * width : 3 * width] += mm(lifted_half, hidden, 0, 0)
        acc_ref[:heads, 3 * width : 3 * width + pair_ref.shape[2]] += mm(bias, normed_out, 1, 0)


def backward_rows(pair_states, bias, win, wout, wb, previous, chunk, chunks, step):
    rows, n, cz = pair_states.shape
    width = wout.shape[0]
    heads = wb.shape[0]
    count = rows // chunks
    step = min(step, count)
    first = chunk * (count // step)
    columns = 3 * width + 2 * cz
    whole = lambda i: (0, 0)
    operands = [pair_states, bias, win, wout, win.T, wout.T, wb]
    specs = [
        pl.BlockSpec((step, n, cz), lambda i: (first + i, 0, 0)),
        pl.BlockSpec((step, heads, n), lambda i: (i, 0, 0)),
    ] + [pl.BlockSpec(a.shape, whole) for a in operands[2:]]
    aliases = {}
    if previous is not None:
        operands += [previous[1], previous[0]]
        specs += [pl.BlockSpec((cz, columns), whole), pl.BlockSpec(memory_space=pl.ANY)]
        aliases = {len(operands) - 1: 0}
    return pl.pallas_call(
        backward_kernel,
        name=f"pair_backward_{chunk}",
        grid=(count // step,),
        in_specs=specs,
        out_specs=[
            pl.BlockSpec((step, n, cz), lambda i: (first + i, 0, 0)),
            pl.BlockSpec((cz, columns), whole),
        ],
        out_shape=[
            jax.ShapeDtypeStruct(pair_states.shape, BF16),
            jax.ShapeDtypeStruct((cz, columns), F32),
        ],
        input_output_aliases=aliases,
        compiler_params=pltpu.CompilerParams(vmem_limit_bytes=VMEM_LIMIT),
        cost_estimate=pl.CostEstimate(
            flops=2 * count * n * cz * (9 * width + 2 * heads) * 2,
            bytes_accessed=count * n * (2 * cz + heads) * 2,
            transcendentals=count * n * width,
        ),
    )(*operands)


def attention_kernel(weight_ref, mask_ref, bias_ref, q_ref, k_ref, v_ref, g_ref,
                     dq_ref, dk_ref, dv_ref, sum_ref, total, att_buf, ds_buf, gh_buf):
    sample = pl.program_id(1)
    scaling = 1.0 / math.sqrt(q_ref.shape[0])
    n = q_ref.shape[1]
    tile = min(n, 128)
    gh_buf[...] = (weight_ref[sample] * g_ref[...].astype(F32)).astype(BF16)
    valid = mask_ref[...] > 0

    @pl.when(sample == 0)
    def _():
        total[...] = jnp.zeros_like(total)

    @pl.loop(0, n // tile)
    def _(i):
        rows = pl.ds(pl.multiple_of(i * tile, tile), tile)
        scores = mm(q_ref[:, rows], k_ref[...], 0, 0) * scaling + bias_ref[rows, :].astype(F32)
        scores = jnp.where(valid, scores, masked_score)
        peak = jnp.max(scores, -1, keepdims=True)
        powers = jnp.exp(scores - peak)
        attention = powers * (1.0 / jnp.sum(powers, -1, keepdims=True))
        att_buf[rows, :] = attention.astype(BF16)
        d_attention = mm(gh_buf[:, rows], v_ref[...], 0, 0)
        inner = jnp.sum(attention * d_attention, -1, keepdims=True)
        d_scores = attention * (d_attention - inner)
        ds_buf[rows, :] = d_scores.astype(BF16)
        total[rows, :] += d_scores

    dv_ref[...] = mm(gh_buf[...], att_buf[...], 1, 0).astype(BF16)
    dq_ref[...] = (mm(k_ref[...], ds_buf[...], 1, 1) * scaling).astype(BF16)
    dk_ref[...] = (mm(q_ref[...], ds_buf[...], 1, 0) * scaling).astype(BF16)

    @pl.when(sample == pl.num_programs(1) - 1)
    def _():
        sum_ref[...] = total[...].astype(BF16)


def attend(weights, mask, bias, queries, keys_in, values_in, grads_in):
    layers, _, samples, depth, n = queries.shape
    vec = pl.BlockSpec((None, None, None, depth, n), lambda b, s: (b, 0, s, 0, 0))
    grid_spec = pl.BlockSpec((None, n, n), lambda b, s: (b, 0, 0))
    return pl.pallas_call(
        attention_kernel,
        name="attention_back",
        grid=(layers, samples),
        in_specs=[
            pl.BlockSpec(memory_space=pltpu.SMEM),
            pl.BlockSpec((1, n), lambda b, s: (0, 0)),
            grid_spec, vec, vec, vec, vec,
        ],
        out_specs=[vec, vec, vec, grid_spec],
        out_shape=[jax.ShapeDtypeStruct(queries.shape, BF16)] * 3
        + [jax.ShapeDtypeStruct((layers, n, n), BF16)],
        scratch_shapes=[
            pltpu.VMEM((n, n), F32),
            pltpu.VMEM((n, n), BF16),
            pltpu.VMEM((n, n), BF16),
            pltpu.VMEM((depth, n), BF16),
        ],
        compiler_params=pltpu.CompilerParams(vmem_limit_bytes=VMEM_LIMIT),
    )(weights, mask, bias, queries, keys_in, values_in, grads_in)


PIECES = 16


def reduce_kernel(devices, part_ref, out_ref, acc, sent, got, full, send_sem, recv_sem, pass_sem, land_sem):
    me = lax.axis_index("tok")
    stages = devices.bit_length() - 1
    half_rows = PIECES // 2
    piece_rows = part_ref.shape[0] // half_rows
    piece_columns = part_ref.shape[1] // 2
    bits = [lax.rem(me // (1 << k), 2) for k in range(stages)]
    partners = [me + (1 - 2 * bits[k]) * (1 << k) for k in range(stages)]
    barrier = pltpu.get_barrier_semaphore()
    for partner in partners:
        pl.semaphore_signal(
            barrier, inc=1, device_id={"tok": partner}, device_id_type=pl.DeviceIdType.MESH
        )
    for half in range(2):
        for band in range(half_rows):
            acc[half * half_rows + band] = part_ref[
                band * piece_rows : (band + 1) * piece_rows,
                half * piece_columns : (half + 1) * piece_columns,
            ]
    pl.semaphore_wait(barrier, stages)

    low = 0
    length = PIECES
    used = 0
    spans = []
    for k in range(stages):
        split = length > 1
        size = length // 2 if split else 1
        away = low + (1 - bits[k]) * size if split else low
        low = low + bits[k] * size if split else low
        sent[used : used + size] = acc[pl.ds(away, size)].astype(BF16)
        copy = pltpu.make_async_remote_copy(
            src_ref=sent.at[pl.ds(used, size)],
            dst_ref=got.at[pl.ds(used, size)],
            send_sem=send_sem.at[k],
            recv_sem=recv_sem.at[k],
            device_id={"tok": partners[k]},
            device_id_type=pl.DeviceIdType.MESH,
        )
        copy.start()
        copy.wait()
        if split:
            acc[pl.ds(low, size)] = acc[pl.ds(low, size)] + got[used : used + size].astype(F32)
            spans.append((k, low, size))
        else:
            acc[pl.ds(low, size)] = sent[used : used + size].astype(F32) + got[
                used : used + size
            ].astype(F32)
        length = size
        used += size

    full[pl.ds(low, length)] = acc[pl.ds(low, length)].astype(BF16)
    for k, start, size in reversed(spans):
        copy = pltpu.make_async_remote_copy(
            src_ref=full.at[pl.ds(start, size)],
            dst_ref=full.at[pl.ds(start, size)],
            send_sem=pass_sem.at[k],
            recv_sem=land_sem.at[k],
            device_id={"tok": partners[k]},
            device_id_type=pl.DeviceIdType.MESH,
        )
        copy.start()
        copy.wait()
    for half in range(2):
        for band in range(half_rows):
            out_ref[
                band * piece_rows : (band + 1) * piece_rows,
                half * piece_columns : (half + 1) * piece_columns,
            ] = full[half * half_rows + band].astype(F32)


def reduce_all(part, devices):
    rows, columns = part.shape
    stages = devices.bit_length() - 1
    piece = (rows // (PIECES // 2), columns // 2)
    slots = 0
    length = PIECES
    for _ in range(stages):
        length = max(length // 2, 1)
        slots += length
    dma = pltpu.SemaphoreType.DMA((stages,))
    return pl.pallas_call(
        functools.partial(reduce_kernel, devices),
        name="weight_reduce",
        in_specs=[pl.BlockSpec(memory_space=pltpu.VMEM)],
        out_specs=pl.BlockSpec(memory_space=pltpu.VMEM),
        out_shape=jax.ShapeDtypeStruct(part.shape, F32),
        scratch_shapes=[
            pltpu.VMEM((PIECES,) + piece, F32),
            pltpu.VMEM((slots,) + piece, BF16),
            pltpu.VMEM((slots,) + piece, BF16),
            pltpu.VMEM((PIECES,) + piece, BF16),
            dma, dma, dma, dma,
        ],
        compiler_params=pltpu.CompilerParams(
            collective_id=0, has_side_effects=True, vmem_limit_bytes=VMEM_LIMIT
        ),
    )(part)


def exchange(x):
    return lax.all_to_all(x, "tok", split_axis=0, concat_axis=0, tiled=True)


def body(
    pair_states,
    weight_in,
    weight_out,
    weight_bias,
    key_mask,
    noise_level,
    query_states,
    key_states,
    value_states,
    output_grad,
):
    rows, n, cz = pair_states.shape
    layers, _, head_count = weight_bias.shape
    width = weight_out.shape[0]
    devices = lax.axis_size("tok")
    groups = devices // head_count
    samples = query_states.shape[2]
    chunks = CHUNKS if rows % CHUNKS == 0 else 1
    part = rows // chunks
    heads = head_count * layers
    wb = jnp.transpose(weight_bias, (2, 0, 1)).reshape(heads, cz)

    arrived = []
    for chunk in range(chunks):
        tiles = forward_rows(pair_states, weight_in, weight_out, wb, chunk, chunks, 2)
        tiles = tiles.reshape(part, head_count, layers, n).transpose(1, 2, 0, 3)
        arrived.append(exchange(jnp.tile(tiles, (groups, 1, 1, 1))))
    bias = jnp.stack(arrived, 2)
    bias = bias.transpose(1, 0, 2, 3, 4).reshape(layers, n, n)

    group = lax.axis_index("tok") // head_count
    weights = sample_weight(lax.dynamic_slice_in_dim(noise_level, group * samples, samples))
    query_grad, key_grad, value_grad, sums = attend(
        weights, key_mask.reshape(1, n), bias,
        query_states, key_states, value_states, output_grad,
    )
    totals = sums.reshape(layers, devices, chunks, part, n)
    returned = [exchange(totals[:, :, chunk].transpose(1, 0, 2, 3)) for chunk in range(chunks)]
    state = None
    for chunk in range(chunks):
        back = returned[chunk]
        if groups > 1:
            back = back.reshape(groups, heads, part, n).astype(F32).sum(0).astype(BF16)
        back = back.reshape(heads, part, n).transpose(1, 0, 2)
        state = backward_rows(
            pair_states, back, weight_in, weight_out, wb, state, chunk, chunks, 2
        )
    pair_grad, acc = state
    acc = reduce_all(acc, devices)
    grad_in = acc[:, : 2 * width]
    grad_out = acc[:, 2 * width : 3 * width].T
    grad_bias = acc[:heads, 3 * width : 3 * width + cz].reshape(head_count, layers, cz)
    grad_bias = grad_bias.transpose(1, 2, 0)
    return (pair_grad, query_grad, key_grad, value_grad, grad_in, grad_out, grad_bias)


def solution(mesh):
    in_specs = (
        P(("job", "tok"), None, None),
        P(),
        P(),
        P(),
        P("job"),
        P("job"),
        P(None, "tok", "job", None, None),
        P(None, "tok", "job", None, None),
        P(None, "tok", "job", None, None),
        P(None, "tok", "job", None, None),
    )
    out_specs = (
        P(("job", "tok"), None, None),
        P(None, "tok", "job", None, None),
        P(None, "tok", "job", None, None),
        P(None, "tok", "job", None, None),
        P("job", None),
        P("job", None),
        P("job", None, None),
    )
    return jax.shard_map(body, mesh=mesh, in_specs=in_specs, out_specs=out_specs, check_vma=False)
```

```python
import functools
import math

import jax
import jax.numpy as jnp
from jax import lax
from jax.experimental import pallas as pl
from jax.experimental.pallas import tpu as pltpu
from jax.sharding import PartitionSpec as P

LEVELS = 200
CHUNKS = 2
VMEM_LIMIT = 56 * 1024 * 1024

sigma_high = 160.0
sigma_low = 0.0004
sigma_data = 16.0
rho_power = 7.0
epsilon = 1e-05
masked_score = -1000000000.0

F32 = jnp.float32
BF16 = jnp.bfloat16


def sample_weight(levels):
    level = levels.astype(F32)
    top_root = sigma_high ** (1.0 / rho_power)
    low_root = sigma_low ** (1.0 / rho_power)
    sigma_level = (top_root + level / (LEVELS - 1) * (low_root - top_root)) ** rho_power
    return (sigma_level * sigma_level + sigma_data * sigma_data) / (sigma_level + sigma_data) ** 2


def normalize(inputs):
    row_mean = jnp.mean(inputs, -1, keepdims=True)
    centered = inputs - row_mean
    variance = jnp.mean(centered * centered, -1, keepdims=True)
    inv_std = lax.rsqrt(variance + epsilon)
    return (centered * inv_std, inv_std)


def norm_back(normed, inv_std, upstream):
    return inv_std * (
        upstream
        - jnp.mean(upstream, -1, keepdims=True)
        - normed * jnp.mean(upstream * normed, -1, keepdims=True)
    )


def mm(a, b, ca, cb):
    return lax.dot_general(a, b, (((ca,), (cb,)), ((), ())), preferred_element_type=F32)


def sigmoid(x):
    return 0.5 * jnp.tanh(0.5 * x) + 0.5


def forward_kernel(pair_ref, win_ref, wout_ref, wb_ref, bias_ref):
    width = wout_ref.shape[0]
    for r in range(pair_ref.shape[0]):
        pair_float = pair_ref[r].astype(F32)
        normed_in = normalize(pair_float)[0].astype(BF16)
        projected = mm(normed_in, win_ref[...], 1, 0)
        gate = projected[:, :width]
        hidden = (gate * sigmoid(gate) * projected[:, width:]).astype(BF16)
        lifted = pair_float + mm(hidden, wout_ref[...], 1, 0)
        normed_out = normalize(lifted)[0].astype(BF16)
        bias_ref[r] = mm(wb_ref[...], normed_out, 1, 1).astype(BF16)


def forward_rows(pair_states, win, wout, wb, chunk, chunks, step):
    rows, n, cz = pair_states.shape
    count = rows // chunks
    step = min(step, count)
    first = chunk * (count // step)
    heads = wb.shape[0]
    return pl.pallas_call(
        forward_kernel,
        name=f"pair_forward_{chunk}",
        grid=(count // step,),
        in_specs=[
            pl.BlockSpec((step, n, cz), lambda i: (first + i, 0, 0)),
            pl.BlockSpec(win.shape, lambda i: (0, 0)),
            pl.BlockSpec(wout.shape, lambda i: (0, 0)),
            pl.BlockSpec(wb.shape, lambda i: (0, 0)),
        ],
        out_specs=pl.BlockSpec((step, heads, n), lambda i: (i, 0, 0)),
        out_shape=jax.ShapeDtypeStruct((count, heads, n), BF16),
        compiler_params=pltpu.CompilerParams(vmem_limit_bytes=VMEM_LIMIT),
        cost_estimate=pl.CostEstimate(
            flops=2 * count * n * cz * (3 * wout.shape[0] + heads) * 2,
            bytes_accessed=count * n * (cz + heads) * 2,
            transcendentals=count * n * wout.shape[0],
        ),
    )(pair_states, win, wout, wb)


def backward_kernel(pair_ref, bias_ref, win_ref, wout_ref, wint_ref, woutt_ref, wb_ref, *rest):
    out_ref, acc_ref = rest[-2:]
    width = wout_ref.shape[0]
    heads = wb_ref.shape[0]

    @pl.when(pl.program_id(0) == 0)
    def _():
        if len(rest) == 4:
            acc_ref[...] = rest[0][...]
        else:
            acc_ref[...] = jnp.zeros_like(acc_ref)

    for r in range(pair_ref.shape[0]):
        pair_float = pair_ref[r].astype(F32)
        xhat, inv_in = normalize(pair_float)
        normed_in = xhat.astype(BF16)
        projected = mm(normed_in, win_ref[...], 1, 0)
        gate = projected[:, :width]
        up = projected[:, width:]
        sg = sigmoid(gate)
        act = gate * sg
        hidden = (act * up).astype(BF16)
        lifted = pair_float + mm(hidden, wout_ref[...], 1, 0)
        yhat, inv_out = normalize(lifted)
        normed_out = yhat.astype(BF16)
        bias = bias_ref[r]
        d_normed = mm(bias, wb_ref[...], 0, 0)
        d_lifted = norm_back(yhat, inv_out, d_normed)
        lifted_half = d_lifted.astype(BF16)
        d_hidden = mm(lifted_half, woutt_ref[...], 1, 0)
        d_gate = (d_hidden * up * (sg + act * (1.0 - sg))).astype(BF16)
        d_up = (d_hidden * act).astype(BF16)
        d_normed_in = mm(d_gate, wint_ref[:width], 1, 0) + mm(d_up, wint_ref[width:], 1, 0)
        out_ref[r] = (d_lifted + norm_back(xhat, inv_in, d_normed_in)).astype(BF16)
        acc_ref[:, :width] += mm(normed_in, d_gate, 0, 0)
        acc_ref[:, width : 2 * width] += mm(normed_in, d_up, 0, 0)
        acc_ref[:, 2 * width : 3 * width] += mm(lifted_half, hidden, 0, 0)
        acc_ref[:heads, 3 * width : 3 * width + pair_ref.shape[2]] += mm(bias, normed_out, 1, 0)


def backward_rows(pair_states, bias, win, wout, wb, previous, chunk, chunks, step):
    rows, n, cz = pair_states.shape
    width = wout.shape[0]
    heads = wb.shape[0]
    count = rows // chunks
    step = min(step, count)
    first = chunk * (count // step)
    columns = 3 * width + 2 * cz
    whole = lambda i: (0, 0)
    operands = [pair_states, bias, win, wout, win.T, wout.T, wb]
    specs = [
        pl.BlockSpec((step, n, cz), lambda i: (first + i, 0, 0)),
        pl.BlockSpec((step, heads, n), lambda i: (i, 0, 0)),
    ] + [pl.BlockSpec(a.shape, whole) for a in operands[2:]]
    aliases = {}
    if previous is not None:
        operands += [previous[1], previous[0]]
        specs += [pl.BlockSpec((cz, columns), whole), pl.BlockSpec(memory_space=pl.ANY)]
        aliases = {len(operands) - 1: 0}
    return pl.pallas_call(
        backward_kernel,
        name=f"pair_backward_{chunk}",
        grid=(count // step,),
        in_specs=specs,
        out_specs=[
            pl.BlockSpec((step, n, cz), lambda i: (first + i, 0, 0)),
            pl.BlockSpec((cz, columns), whole),
        ],
        out_shape=[
            jax.ShapeDtypeStruct(pair_states.shape, BF16),
            jax.ShapeDtypeStruct((cz, columns), F32),
        ],
        input_output_aliases=aliases,
        compiler_params=pltpu.CompilerParams(vmem_limit_bytes=VMEM_LIMIT),
        cost_estimate=pl.CostEstimate(
            flops=2 * count * n * cz * (9 * width + 2 * heads) * 2,
            bytes_accessed=count * n * (2 * cz + heads) * 2,
            transcendentals=count * n * width,
        ),
    )(*operands)


def attention_kernel(weight_ref, mask_ref, bias_ref, q_ref, k_ref, v_ref, g_ref,
                     dq_ref, dk_ref, dv_ref, sum_ref, total, att_buf, ds_buf, gh_buf):
    sample = pl.program_id(1)
    scaling = 1.0 / math.sqrt(q_ref.shape[0])
    n = q_ref.shape[1]
    tile = min(n, 128)
    gh_buf[...] = (weight_ref[sample] * g_ref[...].astype(F32)).astype(BF16)
    valid = mask_ref[...] > 0

    @pl.when(sample == 0)
    def _():
        total[...] = jnp.zeros_like(total)

    @pl.loop(0, n // tile)
    def _(i):
        rows = pl.ds(pl.multiple_of(i * tile, tile), tile)
        scores = mm(q_ref[:, rows], k_ref[...], 0, 0) * scaling + bias_ref[rows, :].astype(F32)
        scores = jnp.where(valid, scores, masked_score)
        peak = jnp.max(scores, -1, keepdims=True)
        powers = jnp.exp(scores - peak)
        attention = powers * (1.0 / jnp.sum(powers, -1, keepdims=True))
        att_buf[rows, :] = attention.astype(BF16)
        d_attention = mm(gh_buf[:, rows], v_ref[...], 0, 0)
        inner = jnp.sum(attention * d_attention, -1, keepdims=True)
        d_scores = attention * (d_attention - inner)
        ds_buf[rows, :] = d_scores.astype(BF16)
        total[rows, :] += d_scores

    dv_ref[...] = mm(gh_buf[...], att_buf[...], 1, 0).astype(BF16)
    dq_ref[...] = (mm(k_ref[...], ds_buf[...], 1, 1) * scaling).astype(BF16)
    dk_ref[...] = (mm(q_ref[...], ds_buf[...], 1, 0) * scaling).astype(BF16)

    @pl.when(sample == pl.num_programs(1) - 1)
    def _():
        sum_ref[...] = total[...].astype(BF16)


def attend(weights, mask, bias, queries, keys_in, values_in, grads_in):
    layers, _, samples, depth, n = queries.shape
    vec = pl.BlockSpec((None, None, None, depth, n), lambda b, s: (b, 0, s, 0, 0))
    grid_spec = pl.BlockSpec((None, n, n), lambda b, s: (b, 0, 0))
    return pl.pallas_call(
        attention_kernel,
        name="attention_back",
        grid=(layers, samples),
        in_specs=[
            pl.BlockSpec(memory_space=pltpu.SMEM),
            pl.BlockSpec((1, n), lambda b, s: (0, 0)),
            grid_spec, vec, vec, vec, vec,
        ],
        out_specs=[vec, vec, vec, grid_spec],
        out_shape=[jax.ShapeDtypeStruct(queries.shape, BF16)] * 3
        + [jax.ShapeDtypeStruct((layers, n, n), BF16)],
        scratch_shapes=[
            pltpu.VMEM((n, n), F32),
            pltpu.VMEM((n, n), BF16),
            pltpu.VMEM((n, n), BF16),
            pltpu.VMEM((depth, n), BF16),
        ],
        compiler_params=pltpu.CompilerParams(vmem_limit_bytes=VMEM_LIMIT),
    )(weights, mask, bias, queries, keys_in, values_in, grads_in)


PIECES = 16


def reduce_kernel(devices, part_ref, out_ref, acc, sent, got, full, send_sem, recv_sem, pass_sem, land_sem):
    me = lax.axis_index("tok")
    stages = devices.bit_length() - 1
    half_rows = PIECES // 2
    piece_rows = part_ref.shape[0] // half_rows
    piece_columns = part_ref.shape[1] // 2
    bits = [lax.rem(me // (1 << k), 2) for k in range(stages)]
    partners = [me + (1 - 2 * bits[k]) * (1 << k) for k in range(stages)]
    barrier = pltpu.get_barrier_semaphore()
    for partner in partners:
        pl.semaphore_signal(
            barrier, inc=1, device_id={"tok": partner}, device_id_type=pl.DeviceIdType.MESH
        )
    for half in range(2):
        for band in range(half_rows):
            acc[half * half_rows + band] = part_ref[
                band * piece_rows : (band + 1) * piece_rows,
                half * piece_columns : (half + 1) * piece_columns,
            ]
    pl.semaphore_wait(barrier, stages)

    low = 0
    length = PIECES
    used = 0
    spans = []
    for k in range(stages):
        split = length > 1
        size = length // 2 if split else 1
        away = low + (1 - bits[k]) * size if split else low
        low = low + bits[k] * size if split else low
        sent[used : used + size] = acc[pl.ds(away, size)].astype(BF16)
        copy = pltpu.make_async_remote_copy(
            src_ref=sent.at[pl.ds(used, size)],
            dst_ref=got.at[pl.ds(used, size)],
            send_sem=send_sem.at[k],
            recv_sem=recv_sem.at[k],
            device_id={"tok": partners[k]},
            device_id_type=pl.DeviceIdType.MESH,
        )
        copy.start()
        copy.wait()
        if split:
            acc[pl.ds(low, size)] = acc[pl.ds(low, size)] + got[used : used + size].astype(F32)
            spans.append((k, low, size))
        else:
            acc[pl.ds(low, size)] = sent[used : used + size].astype(F32) + got[
                used : used + size
            ].astype(F32)
        length = size
        used += size

    full[pl.ds(low, length)] = acc[pl.ds(low, length)].astype(BF16)
    for k, start, size in reversed(spans):
        copy = pltpu.make_async_remote_copy(
            src_ref=full.at[pl.ds(start, size)],
            dst_ref=full.at[pl.ds(start, size)],
            send_sem=pass_sem.at[k],
            recv_sem=land_sem.at[k],
            device_id={"tok": partners[k]},
            device_id_type=pl.DeviceIdType.MESH,
        )
        copy.start()
        copy.wait()
    for half in range(2):
        for band in range(half_rows):
            out_ref[
                band * piece_rows : (band + 1) * piece_rows,
                half * piece_columns : (half + 1) * piece_columns,
            ] = full[half * half_rows + band].astype(F32)


def reduce_all(part, devices):
    rows, columns = part.shape
    stages = devices.bit_length() - 1
    piece = (rows // (PIECES // 2), columns // 2)
    slots = 0
    length = PIECES
    for _ in range(stages):
        length = max(length // 2, 1)
        slots += length
    dma = pltpu.SemaphoreType.DMA((stages,))
    return pl.pallas_call(
        functools.partial(reduce_kernel, devices),
        name="weight_reduce",
        in_specs=[pl.BlockSpec(memory_space=pltpu.VMEM)],
        out_specs=pl.BlockSpec(memory_space=pltpu.VMEM),
        out_shape=jax.ShapeDtypeStruct(part.shape, F32),
        scratch_shapes=[
            pltpu.VMEM((PIECES,) + piece, F32),
            pltpu.VMEM((slots,) + piece, BF16),
            pltpu.VMEM((slots,) + piece, BF16),
            pltpu.VMEM((PIECES,) + piece, BF16),
            dma, dma, dma, dma,
        ],
        compiler_params=pltpu.CompilerParams(
            collective_id=0, has_side_effects=True, vmem_limit_bytes=VMEM_LIMIT
        ),
    )(part)


def exchange(x):
    return lax.all_to_all(x, "tok", split_axis=0, concat_axis=0, tiled=True)


def body(
    pair_states,
    weight_in,
    weight_out,
    weight_bias,
    key_mask,
    noise_level,
    query_states,
    key_states,
    value_states,
    output_grad,
):
    rows, n, cz = pair_states.shape
    layers, _, head_count = weight_bias.shape
    width = weight_out.shape[0]
    devices = lax.axis_size("tok")
    groups = devices // head_count
    samples = query_states.shape[2]
    chunks = CHUNKS if rows % CHUNKS == 0 else 1
    part = rows // chunks
    heads = head_count * layers
    wb = jnp.transpose(weight_bias, (2, 0, 1)).reshape(heads, cz)

    arrived = []
    for chunk in range(chunks):
        tiles = forward_rows(pair_states, weight_in, weight_out, wb, chunk, chunks, 2)
        tiles = tiles.reshape(part, head_count, layers, n).transpose(1, 2, 0, 3)
        arrived.append(exchange(jnp.tile(tiles, (groups, 1, 1, 1))))
    bias = jnp.stack(arrived, 2)
    bias = bias.transpose(1, 0, 2, 3, 4).reshape(layers, n, n)

    group = lax.axis_index("tok") // head_count
    weights = sample_weight(lax.dynamic_slice_in_dim(noise_level, group * samples, samples))
    query_grad, key_grad, value_grad, sums = attend(
        weights, key_mask.reshape(1, n), bias,
        query_states, key_states, value_states, output_grad,
    )
    totals = sums.reshape(layers, devices, chunks, part, n)
    returned = []
    for chunk in range(chunks):
        outgoing = totals[:, :, chunk].transpose(1, 0, 2, 3)
        if returned:
            returned[-1], outgoing = lax.optimization_barrier((returned[-1], outgoing))
        returned.append(exchange(outgoing))
    state = None
    for chunk in range(chunks):
        back = returned[chunk]
        if groups > 1:
            back = back.reshape(groups, heads, part, n).astype(F32).sum(0).astype(BF16)
        back = back.reshape(heads, part, n).transpose(1, 0, 2)
        state = backward_rows(
            pair_states, back, weight_in, weight_out, wb, state, chunk, chunks, 2
        )
    pair_grad, acc = state
    acc = reduce_all(acc, devices)
    grad_in = acc[:, : 2 * width]
    grad_out = acc[:, 2 * width : 3 * width].T
    grad_bias = acc[:heads, 3 * width : 3 * width + cz].reshape(head_count, layers, cz)
    grad_bias = grad_bias.transpose(1, 2, 0)
    return (pair_grad, query_grad, key_grad, value_grad, grad_in, grad_out, grad_bias)


def solution(mesh):
    in_specs = (
        P(("job", "tok"), None, None),
        P(),
        P(),
        P(),
        P("job"),
        P("job"),
        P(None, "tok", "job", None, None),
        P(None, "tok", "job", None, None),
        P(None, "tok", "job", None, None),
        P(None, "tok", "job", None, None),
    )
    out_specs = (
        P(("job", "tok"), None, None),
        P(None, "tok", "job", None, None),
        P(None, "tok", "job", None, None),
        P(None, "tok", "job", None, None),
        P("job", None),
        P("job", None),
        P("job", None, None),
    )
    return jax.shard_map(body, mesh=mesh, in_specs=in_specs, out_specs=out_specs, check_vma=False)
```
